128 devices in a mesh: wide: 16 (over y, z_hi, core), narrow: 8 (over z_lo, x).
Axes of the slice: x: 4, y: 4, z: 4 (z_hi: 2, z_lo: 2; z = z_hi * 2 + z_lo), core: 2. Of those that a mesh axis runs over, the one named last changes fastest.
Arguments:
- pressure: float32 [64, 512, 512], P('wide', 'narrow'), may hold values from -6 to 6
- source: float32 [64, 512, 512], P('wide', 'narrow'), may hold values from -6 to 6
- permeability: float32 [64, 512, 512], P('wide', 'narrow'), may hold values from 0.1 to 10
- active_mask: int32 [64, 512, 512], P('wide', 'narrow'), may hold values 0 or 1
Outputs:
- smoothed_pressure: float32 [64, 512, 512], P('wide', 'narrow')
The draws below stay inside these ranges and needn't reach their ends.
Inputs may be any that keep to these rules, and one draw needn't show every extreme that they name: `active_mask`: 1 marks an active cell.
All inputs are finite; a program needn't handle non-finite values. No bound on the sum of `active_mask` on one device may be relied on, other than what follows from the above.
Results may differ from the reference program's by a relative error of at most 0.00002.
Values sent between devices are 32-bit elements; how exact they have to be, the bound alone decides.
A program may use at most 256 MiB of HBM per device.

```python
import math
import jax
import jax.numpy as jnp

CY = 512
NX = 64
NZ = 512


def place_ends(array, rng, smallest, largest):
    longest = array.shape.index(max(array.shape))
    spots = []
    for shift in (0, 1):
        where = [jax.random.randint(jax.random.fold_in(rng, axis), (), 0, length) for axis, length in enumerate(array.shape)]
        where[longest] = (where[longest] + shift) % array.shape[longest]
        spots.append(tuple(where))
    return array.at[spots[0]].set(smallest).at[spots[1]].set(largest)


def block_scale(own_key, shape, shards, smallest, largest):
    def one(position, parts):
        steps = jax.random.uniform(jax.random.fold_in(jax.random.fold_in(own_key, 6), position), (parts,), jnp.float32, smallest / len(shards), largest / len(shards))
        return jnp.repeat(jnp.exp(steps), shape[position] // parts).reshape((-1,) + (1,) * (len(shape) - position - 1))

    gain = one(*shards[0])
    for cut in shards[1:]:
        gain = gain * one(*cut)
    return gain


def noise(key, dims, spread, reach, pieces=(), held_as=jnp.bfloat16):
    array = jax.random.normal(key, dims, jnp.float32) * spread
    if len(pieces) > 0:
        array = block_scale(key, dims, pieces, -0.22, 0.18) * array
    return jnp.clip(array, min=-reach, max=reach).astype(held_as)


def setup_inputs(seed: int = 0) -> dict:
    key_of = jax.random.split(jax.random.key(seed), 5)
    return {
        "pressure": noise(key_of[0], (NX, NZ, CY), 1.0, 6.0, ((0, 16), (1, 8)), jnp.float32),
        "source": noise(key_of[1], (NX, NZ, CY), 1.0, 6.0, ((0, 16), (1, 8)), jnp.float32),
        "permeability": jnp.clip(jnp.exp(math.log(10.0) - 4.6051702 * jax.random.uniform(key_of[2], (NX, NZ, CY), jnp.float32) ** block_scale(key_of[2], (NX, NZ, CY), ((0, 16), (1, 8)), -0.2, 0.2)), 0.1, 10.0),
        "active_mask": place_ends((jax.random.randint(key_of[3], (NX, NZ, CY), 0, 8) < 7).astype(jnp.int32), jax.random.fold_in(key_of[3], 1), 0, 1),
    }


RELAX_WEIGHT = 0.8
STORE_COEFF = 0.5
FLOOR_SUM = 0.1
NEIGHBOURS = ((0, 1, 1), (2, 1, 1), (1, 0, 1), (1, 2, 1), (1, 1, 0), (1, 1, 2))


def relax_cells(padded_field, padded_perm, source, active, spacing):
    size_x, size_z, size_y = source.shape
    field_pad = jnp.pad(padded_field, ((0, 0), (0, 0), (1, 1)))
    perm_pad = jnp.pad(padded_perm, ((0, 0), (0, 0), (1, 1)))
    centre_field = field_pad[1:size_x + 1, 1:size_z + 1, 1:size_y + 1]
    centre_perm = perm_pad[1:size_x + 1, 1:size_z + 1, 1:size_y + 1]
    flux_sum = jnp.zeros(source.shape, jnp.float32)
    weight = jnp.zeros(source.shape, jnp.float32)
    for off_x, off_z, off_y in NEIGHBOURS:
        near_field = field_pad[off_x:off_x + size_x, off_z:off_z + size_z, off_y:off_y + size_y]
        near_perm = perm_pad[off_x:off_x + size_x, off_z:off_z + size_z, off_y:off_y + size_y]
        conduct = 2.0 * centre_perm * near_perm / jnp.maximum(centre_perm + near_perm, FLOOR_SUM)
        flux_sum = flux_sum + conduct * (centre_field - near_field)
        weight = weight + conduct
    storage = STORE_COEFF * spacing ** 3
    residual = active * (source - storage * centre_field - spacing * flux_sum)
    updated = active * (centre_field + RELAX_WEIGHT * residual / (storage + spacing * weight))
    return updated, residual


def pad_plane(values):
    return jnp.pad(values, ((1, 1), (1, 1), (0, 0)))


def coarsen_sum(values):
    size_x, size_z, size_y = values.shape
    return values.reshape(size_x // 2, 2, size_z // 2, 2, size_y // 2, 2).sum(axis=(1, 3, 5))


def coarsen_max(values):
    size_x, size_z, size_y = values.shape
    return values.reshape(size_x // 2, 2, size_z // 2, 2, size_y // 2, 2).max(axis=(1, 3, 5))


def refine(values):
    return jnp.repeat(jnp.repeat(jnp.repeat(values, 2, 0), 2, 1), 2, 2)


def reference(pressure, source, permeability, active_mask):
    fine_active = active_mask.astype(jnp.float32)
    fine_perm = permeability * fine_active
    fine_padm = pad_plane(fine_perm)
    fine_field = pressure
    for sweep_index in range(2):
        fine_field, unused = relax_cells(pad_plane(fine_field), fine_padm, source, fine_active, 1.0)
    unused, fine_resid = relax_cells(pad_plane(fine_field), fine_padm, source, fine_active, 1.0)
    mid_active = coarsen_max(fine_active)
    mid_raw = coarsen_sum(permeability) * 0.125
    mid_perm = mid_raw * mid_active
    mid_source = mid_active * coarsen_sum(fine_resid)
    mid_padm = pad_plane(mid_perm)
    mid_field = jnp.zeros(mid_source.shape, jnp.float32)
    for sweep_index in range(2):
        mid_field, unused = relax_cells(pad_plane(mid_field), mid_padm, mid_source, mid_active, 2.0)
    unused, mid_resid = relax_cells(pad_plane(mid_field), mid_padm, mid_source, mid_active, 2.0)
    coarse_active = coarsen_max(mid_active)
    coarse_perm = coarsen_sum(mid_raw) * 0.125 * coarse_active
    coarse_source = coarse_active * coarsen_sum(mid_resid)
    coarse_padm = pad_plane(coarse_perm)
    coarse_field = jnp.zeros(coarse_source.shape, jnp.float32)
    for sweep_index in range(4):
        coarse_field, unused = relax_cells(pad_plane(coarse_field), coarse_padm, coarse_source, coarse_active, 4.0)
    mid_field = mid_field + mid_active * refine(coarse_field)
    mid_field, unused = relax_cells(pad_plane(mid_field), mid_padm, mid_source, mid_active, 2.0)
    fine_field = fine_field + fine_active * refine(mid_field)
    fine_field, unused = relax_cells(pad_plane(fine_field), fine_padm, source, fine_active, 1.0)
    return fine_field
```

```python
import functools

import jax
import jax.numpy as jnp
from jax import lax
from jax.experimental import pallas as pl
from jax.experimental.pallas import tpu as pltpu
from jax.sharding import PartitionSpec as P

FLOOR_SUM = 0.1
LANES = 128
F32 = jnp.float32
MESH = pl.DeviceIdType.MESH

FINE_X, FINE_Z = 1, 8
MID_X, MID_Z = 2, 16
COARSE_X, COARSE_Z = 4, 16
REACH = 4


def y_next(values):
    rolled = pltpu.roll(values, LANES - 1, 2)
    if values.shape[0] == 1:
        return rolled
    lane = lax.broadcasted_iota(jnp.int32, values.shape, 2)
    return jnp.where(lane == LANES - 1, jnp.concatenate([rolled[1:], rolled[:1]], 0), rolled)


def y_prev(values):
    rolled = pltpu.roll(values, 1, 2)
    if values.shape[0] == 1:
        return rolled
    lane = lax.broadcasted_iota(jnp.int32, values.shape, 2)
    return jnp.where(lane == 0, jnp.concatenate([rolled[-1:], rolled[:-1]], 0), rolled)


def conduct(left, right, spacing):
    return (2.0 * spacing) * left * right / jnp.maximum(left + right, FLOOR_SUM)


class Level:
    def __init__(self, spacing, perm, tx, tz, ty, diag, inv):
        self.spacing, self.storage = spacing, 0.5 * spacing**3
        self.perm, self.tx, self.tz, self.ty = perm, tx, tz, ty
        self.diag, self.inv = diag, inv

    def make_tx(self, plane, row, rows):
        at = pl.ds(row, rows)
        self.tx[plane, :, at, :] = conduct(
            self.perm[plane - 1, :, at, :], self.perm[plane, :, at, :], self.spacing
        )

    def make_tz(self, plane, row, rows):
        self.tz[plane, :, pl.ds(row, rows), :] = conduct(
            self.perm[plane, :, pl.ds(row - 1, rows), :],
            self.perm[plane, :, pl.ds(row, rows), :],
            self.spacing,
        )

    def make_ty(self, plane, row, rows):
        here = self.perm[plane, :, pl.ds(row, rows), :]
        lane = lax.broadcasted_iota(jnp.int32, here.shape, 2)
        block = lax.broadcasted_iota(jnp.int32, here.shape, 0)
        last = (lane == LANES - 1) & (block == here.shape[0] - 1)
        value = conduct(here, y_next(here), self.spacing)
        self.ty[plane, :, pl.ds(row, rows), :] = jnp.where(last, 0.0, value)

    def make_diag(self, plane, row, rows):
        at, after = pl.ds(row, rows), pl.ds(row + 1, rows)
        along = self.ty[plane, :, at, :]
        total = self.storage + self.tx[plane, :, at, :] + self.tx[plane + 1, :, at, :]
        total = total + self.tz[plane, :, at, :] + self.tz[plane, :, after, :]
        total = total + along + y_prev(along)
        if self.diag is not None:
            self.diag[plane, :, at, :] = total
        self.inv[plane, :, at, :] = jnp.where(self.perm[plane, :, at, :] > 0.0, 0.8 / total, 0.0)

    def flow(self, field, plane, row, rows):
        at, after = pl.ds(row, rows), pl.ds(row + 1, rows)
        here = field[plane, :, at, :]
        along = self.ty[plane, :, at, :]
        total = self.tx[plane, :, at, :] * field[plane - 1, :, at, :]
        total = total + self.tx[plane + 1, :, at, :] * field[plane + 1, :, at, :]
        total = total + self.tz[plane, :, at, :] * field[plane, :, pl.ds(row - 1, rows), :]
        total = total + self.tz[plane, :, after, :] * field[plane, :, after, :]
        total = total + along * y_next(here) + y_prev(along * here)
        return here, total


def take(values, index):
    return jnp.take_along_axis(values, index, axis=1, mode="promise_in_bounds")


def coarsen(ref, plane, block, row, rows):
    lane = lax.broadcasted_iota(jnp.int32, (rows, LANES), 1)
    index = lax.rem(2 * lane, LANES)
    parts = []
    for half in (0, 1):
        total = None
        for step_x in (0, 1):
            for step_z in (0, 1):
                piece = ref[plane + step_x, 2 * block + half, pl.ds(row + step_z, rows, stride=2), :]
                total = piece if total is None else total + piece
        parts.append(take(total + pltpu.roll(total, LANES - 1, 1), index))
    return jnp.where(lane < LANES // 2, parts[0], parts[1])


def refine_rows(target, target_plane, target_block, values):
    rows = values.shape[0]
    lane = lax.broadcasted_iota(jnp.int32, values.shape, 1)
    spread = take(values, (LANES // 2) * (target_block % 2) + lane // 2)
    target[target_plane, target_block, pl.ds(0, rows, stride=2), :] = spread
    target[target_plane, target_block, pl.ds(1, rows, stride=2), :] = spread


def kernel(
    n_wide, n_narrow,
    pressure, source, permeability, active_mask, out,
    raw, act, rhs, v0, v1, v2, v3, perm, tx, tz, ty, diag, inv, resid,
    zs1, zr1, zs2, zr2, zs3, zr3,
    m_raw, m_perm, m_tx, m_tz, m_ty, m_diag, m_inv, m_rhs, m_f1, m_f2, m_u, m_fin, m_refx, m_refz, m_res, rc, rf,
    c_perm, c_tx, c_tz, c_ty, c_inv, c_f1, c_f2, c_f3, c_f4,
    load_sem, send_sem, recv_sem,
):
    wide, narrow = lax.axis_index("wide"), lax.axis_index("narrow")
    fine = Level(1.0, perm, tx, tz, ty, diag, inv)
    mid = Level(2.0, m_perm, m_tx, m_tz, m_ty, m_diag, m_inv)
    coarse = Level(4.0, c_perm, c_tx, c_tz, c_ty, None, c_inv)
    slots = [0]

    def exists(dx, dz):
        ok = None
        for step, here, count in ((dx, wide, n_wide), (dz, narrow, n_narrow)):
            if step == 0:
                continue
            one = here + step < count if step > 0 else here + step >= 0
            ok = one if ok is None else ok & one
        return ok

    class Swap:
        def __init__(self, dx, dz, src, dst):
            slot = slots[0]
            slots[0] += 1
            self.ok, self.back = exists(dx, dz), exists(-dx, -dz)
            self.copy = pltpu.make_async_remote_copy(
                src_ref=src, dst_ref=dst, send_sem=send_sem.at[slot], recv_sem=recv_sem.at[slot],
                device_id=(wide + dx, narrow + dz), device_id_type=MESH,
            )

        def start(self):
            pl.when(self.ok)(self.copy.start)

        def wait_recv(self):
            pl.when(self.back)(self.copy.wait_recv)

        def wait_send(self):
            pl.when(self.ok)(self.copy.wait_send)

    everyone = []

    def swaps(items):
        made = [Swap(*item) for item in items]
        everyone.extend(made)
        return made

    def start(group):
        for one in group:
            one.start()

    def wait(group):
        for one in group:
            one.wait_recv()

    peers = [(dx, dz) for dx in range(-REACH, REACH + 1) for dz in (-1, 0, 1) if (dx, dz) != (0, 0)]

    loads = []
    for which, (src, dst) in enumerate(
        ((permeability, raw), (active_mask, act), (pressure, v0), (source, rhs))
    ):
        for block in range(4):
            into = dst.at[pl.ds(1, 4), block, pl.ds(8, 64), :] if dst is v0 else dst.at[:, block, :, :]
            copy = pltpu.make_async_copy(
                src.at[:, :, pl.ds(block * LANES, LANES)], into, load_sem.at[which * 4 + block]
            )
            copy.start()
            loads.append(copy)

    for ref in (m_perm, m_f1, m_refx, m_refz, c_perm, c_f1, zr1, zr2, zr3):
        ref[...] = jnp.zeros(ref.shape, F32)
    for ref in (m_u, m_f2, c_f2, c_f3):
        ref[...] = jnp.zeros(ref.shape, F32)

    barrier = pltpu.get_barrier_semaphore()
    for dx, dz in peers:
        @pl.when(exists(dx, dz))
        def _():
            pl.semaphore_signal(barrier, inc=1, device_id=(wide + dx, narrow + dz), device_id_type=MESH)

    low_edge, high_edge = wide == 0, wide == n_wide - 1
    for plane, edge in ((0, low_edge), (5, high_edge)):
        @pl.when(edge)
        def _():
            for ref in (perm, v0, v1, v2):
                ref[plane] = jnp.zeros(ref.shape[1:], F32)

    def chunks(first, last, body):
        def step(k, carry):
            body(pl.multiple_of(k * 8, 8))
            return carry
        lax.fori_loop(first // 8, last // 8, step, 0)

    for copy in loads[:8]:
        copy.wait()

    def mask_perm(row):
        for plane in range(4):
            value = raw[plane, :, pl.ds(row, 8), :] * act[plane, :, pl.ds(row, 8), :].astype(F32)
            perm[plane + 1, :, pl.ds(row + 8, 8), :] = value

    chunks(0, 64, mask_perm)
    for copy in loads[8:12]:
        copy.wait()

    def pack(target, field):
        for side, row in ((0, 8), (1, 71)):
            for plane in range(4):
                for block in range(4):
                    target[side, pl.ds(plane * 4 + block, 1), :] = field[plane + 1, block, pl.ds(row, 1), :]

    def unpack(field, buffer):
        for side, row in ((0, 7), (1, 72)):
            for plane in range(4):
                for block in range(4):
                    field[plane + 1, block, pl.ds(row, 1), :] = buffer[side, pl.ds(plane * 4 + block, 1), :]

    def fine_x(field):
        rows = pl.ds(8, 64)
        return swaps([
            (-1, 0, field.at[1, :, rows, :], field.at[5, :, rows, :]),
            (1, 0, field.at[4, :, rows, :], field.at[0, :, rows, :]),
        ])

    def fine_z(send, recv):
        return swaps([(0, -1, send.at[0], recv.at[1]), (0, 1, send.at[1], recv.at[0])])

    pack(zs1.at[0], perm)
    pack(zs1.at[1], v0)

    count_x = jnp.minimum(wide, REACH) + jnp.minimum(n_wide - 1 - wide, REACH) + 1
    count_z = jnp.minimum(narrow, 1) + jnp.minimum(n_narrow - 1 - narrow, 1) + 1
    pl.semaphore_wait(barrier, count_x * count_z - 1)

    perm_x, v0_x = fine_x(perm), fine_x(v0)
    perm_z = fine_z(zs1.at[0], zr1.at[0])
    v0_z = fine_z(zs1.at[1], zr1.at[1])
    start(perm_x + v0_x + perm_z + v0_z)

    for plane in range(2):
        for block in range(2):
            value = coarsen(raw, 2 * plane, block, 0, 32) * 0.125
            m_raw[plane, block] = value
            some = coarsen(perm, 2 * plane + 1, block, 8, 32) > 0.0
            m_perm[plane + 2, block, pl.ds(16, 32), :] = jnp.where(some, value, 0.0)

    def mid_swaps(ref):
        own, low, high = pl.ds(16, 32), pl.ds(16, 8), pl.ds(40, 8)
        below, above = pl.ds(8, 8), pl.ds(48, 8)
        two = pl.ds(2, 2)
        return swaps([
            (-1, 0, ref.at[two, :, own, :], ref.at[pl.ds(4, 2), :, own, :]),
            (1, 0, ref.at[two, :, own, :], ref.at[pl.ds(0, 2), :, own, :]),
            (0, -1, ref.at[two, :, low, :], ref.at[two, :, above, :]),
            (0, 1, ref.at[two, :, high, :], ref.at[two, :, below, :]),
            (-1, -1, ref.at[2, :, low, :], ref.at[4, :, above, :]),
            (-1, 1, ref.at[2, :, high, :], ref.at[4, :, below, :]),
            (1, -1, ref.at[3, :, low, :], ref.at[1, :, above, :]),
            (1, 1, ref.at[3, :, high, :], ref.at[1, :, below, :]),
        ])

    def coarse_swaps(ref):
        mine = {0: pl.ds(16, 16), -1: pl.ds(16, 8), 1: pl.ds(24, 8)}
        theirs = {0: pl.ds(16, 16), -1: pl.ds(32, 8), 1: pl.ds(8, 8)}
        return swaps([
            (dx, dz, ref.at[4, :, mine[dz], :], ref.at[4 - dx, :, theirs[dz], :])
            for dx, dz in sorted(peers, key=lambda one: -abs(one[0]))
        ])

    mid_perm_swaps = mid_swaps(m_perm)
    start(mid_perm_swaps)
    some = coarsen(m_perm, 2, 0, 16, 16) > 0.0
    value = coarsen(m_raw, 0, 0, 0, 16) * 0.125
    c_perm[4, 0, pl.ds(16, 16), :] = jnp.where(some, value, 0.0)
    coarse_perm_swaps = coarse_swaps(c_perm)
    start(coarse_perm_swaps)

    def inner(row):
        for plane in range(1, 5):
            fine.make_ty(plane, row, 8)
            if plane > 1:
                fine.make_tx(plane, row, 8)

    chunks(8, 72, inner)

    def inner_z(row):
        for plane in range(1, 5):
            fine.make_tz(plane, row, 8)

    chunks(16, 72, inner_z)

    wait(perm_z + v0_z)
    unpack(perm, zr1.at[0])
    unpack(v0, zr1.at[1])
    inner_z(8)
    inner_z(72)
    for copy in loads[12:]:
        copy.wait()
    chunks(8, 72, lambda row: [fine.make_diag(plane, row, 8) for plane in (2, 3)])

    def relax(old, new, planes, first):
        def body(row):
            at = pl.ds(row, 8)
            for plane in planes:
                here, total = fine.flow(old, plane, row, 8)
                if first:
                    here = jnp.where(perm[plane, :, at, :] > 0.0, here, 0.0)
                force = rhs[plane - 1, :, pl.ds(row - 8, 8), :] + total
                new[plane, :, at, :] = 0.2 * here + inv[plane, :, at, :] * force
        chunks(8, 72, body)

    wait(perm_x)

    def outer(row):
        fine.make_tx(1, row, 8)
        fine.make_tx(5, row, 8)
        fine.make_diag(1, row, 8)
        fine.make_diag(4, row, 8)

    chunks(8, 72, outer)
    wait(v0_x)

    def sweep(old, new, first, send, recv):
        relax(old, new, (1, 4), first)
        by_x = fine_x(new)
        start(by_x)
        relax(old, new, (2, 3), first)
        pack(send, new)
        by_z = fine_z(send, recv)
        start(by_z)
        return by_x, by_z

    v1_x, v1_z = sweep(v0, v1, True, zs2, zr2)

    wait(mid_perm_swaps)
    for plane in range(1, 6):
        mid.make_tx(plane, 8, 48)
    for plane in range(1, 5):
        mid.make_ty(plane, 8, 48)
        mid.make_tz(plane, 8, 56)
        mid.make_diag(plane, 8, 48)

    wait(v1_z)
    unpack(v1, zr2)
    wait(v1_x)
    v2_x, v2_z = sweep(v1, v2, False, zs3, zr3)

    wait(coarse_perm_swaps)
    for plane in range(1, 9):
        coarse.make_tx(plane, 8, 32)
    for plane in range(1, 8):
        coarse.make_ty(plane, 8, 32)
        coarse.make_tz(plane, 8, 40)
        coarse.make_diag(plane, 8, 32)

    def residual(planes):
        def body(row):
            at = pl.ds(row, 8)
            for plane in planes:
                here, total = fine.flow(v2, plane, row, 8)
                value = rhs[plane - 1, :, pl.ds(row - 8, 8), :] + total - diag[plane, :, at, :] * here
                resid[plane - 1, :, pl.ds(row - 8, 8), :] = jnp.where(perm[plane, :, at, :] > 0.0, value, 0.0)
        chunks(8, 72, body)

    wait(v2_z)
    unpack(v2, zr3)
    residual((2, 3))
    wait(v2_x)
    residual((1, 4))

    own = pl.ds(16, 32)
    for plane in range(2):
        for block in range(2):
            value = coarsen(resid, 2 * plane, block, 0, 32)
            value = jnp.where(m_perm[plane + 2, block, own, :] > 0.0, value, 0.0)
            m_rhs[plane, block] = value
            m_f1[plane + 2, block, own, :] = m_inv[plane + 2, block, own, :] * value
    mid_f1_swaps = mid_swaps(m_f1)
    start(mid_f1_swaps)
    wait(mid_f1_swaps)
    for plane in range(1, 5):
        here, total = mid.flow(m_f1, plane, 8, 48)
        m_f2[plane, :, pl.ds(8, 48), :] = 1.2 * here + m_inv[plane, :, pl.ds(8, 48), :] * total
    for plane in range(2):
        here, total = mid.flow(m_f2, plane + 2, 16, 32)
        value = m_rhs[plane] + total - m_diag[plane + 2, :, own, :] * here
        m_res[plane] = jnp.where(m_perm[plane + 2, :, own, :] > 0.0, value, 0.0)

    here = pl.ds(16, 16)
    value = coarsen(m_res, 0, 0, 0, 16)
    c_f1[4, 0, here, :] = c_inv[4, 0, here, :] * value
    coarse_f1_swaps = coarse_swaps(c_f1)
    start(coarse_f1_swaps)
    tall = pl.ds(8, 48)
    two = pl.ds(2, 2)
    mid_f2_swaps = swaps([
        (-1, 0, m_f2.at[two, :, tall, :], m_refx.at[1]),
        (1, 0, m_f2.at[two, :, tall, :], m_refx.at[0]),
        (0, -1, m_f2.at[two, :, pl.ds(16, 8), :], m_refz.at[1]),
        (0, 1, m_f2.at[two, :, pl.ds(40, 8), :], m_refz.at[0]),
    ])
    start(mid_f2_swaps)
    wait(coarse_f1_swaps)
    body = pl.ds(8, 32)
    for old, new, first, last in ((c_f1, c_f2, 1, 7), (c_f2, c_f3, 2, 6), (c_f3, c_f4, 3, 5)):
        for plane in range(first, last + 1):
            value, total = coarse.flow(old, plane, 8, 32)
            value = 1.2 * value if old is c_f1 else 0.2 * value + c_f1[plane, :, body, :]
            new[plane, :, body, :] = value + c_inv[plane, :, body, :] * total

    for plane in range(3):
        for block in range(2):
            refine_rows(rc, plane, block, c_f4[plane + 3, 0, body, :])
    wait(mid_f2_swaps)
    for plane in range(6):
        for block in range(2):
            add = jnp.where(m_perm[plane, block, tall, :] > 0.0, rc[plane // 2, block, tall, :], 0.0)
            if plane in (2, 3):
                base = jnp.concatenate([
                    m_refz[0, plane - 2, block], m_f2[plane, block, own, :], m_refz[1, plane - 2, block]
                ], 0)
            else:
                base = m_refx[plane // 4, plane % 2, block]
            m_u[plane, block, tall, :] = base + add
    for plane in range(1, 5):
        value, total = mid.flow(m_u, plane, 8, 48)
        value = 0.2 * value + m_f1[plane, :, tall, :] + m_inv[plane, :, tall, :] * total
        m_fin[plane, :, tall, :] = value

    for plane in range(4):
        for block in range(4):
            refine_rows(rf, plane, block, m_fin[plane + 1, block // 2, pl.ds(12, 40), :])

    def correct(row):
        at = pl.ds(row, 8)
        for plane in range(6):
            add = jnp.where(perm[plane, :, at, :] > 0.0, rf[(plane + 1) // 2, :, at, :], 0.0)
            v3[plane, :, at, :] = v2[plane, :, at, :] + add

    chunks(0, 80, correct)

    def finish(row):
        at = pl.ds(row, 8)
        for plane in range(1, 5):
            value, total = fine.flow(v3, plane, row, 8)
            force = rhs[plane - 1, :, pl.ds(row - 8, 8), :] + total
            value = 0.2 * value + inv[plane, :, at, :] * force
            for block in range(4):
                out[plane - 1, pl.ds(pl.multiple_of(row - 8, 8), 8), pl.ds(block * LANES, LANES)] = value[block]

    chunks(8, 72, finish)
    for one in everyone:
        one.wait_send()


def per_device(n_wide, n_narrow, pressure, source, permeability, active_mask):
    def vmem(*shape, dtype=F32):
        return pltpu.VMEM(shape, dtype)

    fine_pad, fine_own = (6, 4, 80, LANES), (4, 4, 64, LANES)
    mid_pad, mid_own = (6, 2, 64, LANES), (2, 2, 32, LANES)
    coarse_pad = (9, 1, 48, LANES)
    scratch = [vmem(*fine_own), vmem(*fine_own, dtype=jnp.int32), vmem(*fine_own)]
    scratch += [vmem(*fine_pad) for _ in range(10)] + [vmem(*fine_own)]
    scratch += [vmem(2, 2, 16, LANES), vmem(2, 2, 16, LANES)] + [vmem(2, 16, LANES) for _ in range(4)]
    scratch += [vmem(*mid_own)] + [vmem(*mid_pad) for _ in range(6)] + [vmem(*mid_own)]
    scratch += [vmem(*mid_pad) for _ in range(4)]
    scratch += [vmem(2, 2, 2, 48, LANES), vmem(2, 2, 2, 8, LANES), vmem(*mid_own)]
    scratch += [vmem(3, 2, 64, LANES), vmem(4, 4, 80, LANES)]
    scratch += [vmem(*coarse_pad) for _ in range(9)]
    scratch += [pltpu.SemaphoreType.DMA((16,)), pltpu.SemaphoreType.DMA((96,)), pltpu.SemaphoreType.DMA((96,))]
    return pl.pallas_call(
        functools.partial(kernel, n_wide, n_narrow),
        out_shape=jax.ShapeDtypeStruct(pressure.shape, F32),
        in_specs=[pl.BlockSpec(memory_space=pl.ANY)] * 4,
        out_specs=pl.BlockSpec(memory_space=pltpu.VMEM),
        scratch_shapes=scratch,
        compiler_params=pltpu.CompilerParams(
            collective_id=0, has_side_effects=True, vmem_limit_bytes=48 * 1024 * 1024
        ),
        name="vcycle",
    )(pressure, source, permeability, active_mask)


def solution(mesh):
    spec = P("wide", "narrow", None)
    return jax.shard_map(
        functools.partial(per_device, mesh.shape["wide"], mesh.shape["narrow"]),
        mesh=mesh, in_specs=(spec,) * 4, out_specs=spec, check_vma=False,
    )
```

```python
import functools

import jax
import jax.numpy as jnp
from jax import lax
from jax.experimental import pallas as pl
from jax.experimental.pallas import tpu as pltpu
from jax.sharding import PartitionSpec as P

FLOOR_SUM = 0.1
LANES = 128
F32 = jnp.float32
MESH = pl.DeviceIdType.MESH

FINE_X, FINE_Z = 1, 8
MID_X, MID_Z = 2, 16
COARSE_X, COARSE_Z = 4, 16
REACH = 4


def y_next(values):
    rolled = pltpu.roll(values, LANES - 1, 2)
    if values.shape[0] == 1:
        return rolled
    lane = lax.broadcasted_iota(jnp.int32, values.shape, 2)
    return jnp.where(lane == LANES - 1, jnp.concatenate([rolled[1:], rolled[:1]], 0), rolled)


def y_prev(values):
    rolled = pltpu.roll(values, 1, 2)
    if values.shape[0] == 1:
        return rolled
    lane = lax.broadcasted_iota(jnp.int32, values.shape, 2)
    return jnp.where(lane == 0, jnp.concatenate([rolled[-1:], rolled[:-1]], 0), rolled)


def conduct(left, right, spacing):
    return (2.0 * spacing) * left * right / jnp.maximum(left + right, FLOOR_SUM)


class Level:
    def __init__(self, spacing, perm, tx, tz, ty, diag, inv):
        self.spacing, self.storage = spacing, 0.5 * spacing**3
        self.perm, self.tx, self.tz, self.ty = perm, tx, tz, ty
        self.diag, self.inv = diag, inv

    def make_tx(self, plane, row, rows):
        at = pl.ds(row, rows)
        self.tx[plane, :, at, :] = conduct(
            self.perm[plane - 1, :, at, :], self.perm[plane, :, at, :], self.spacing
        )

    def make_tz(self, plane, row, rows):
        self.tz[plane, :, pl.ds(row, rows), :] = conduct(
            self.perm[plane, :, pl.ds(row - 1, rows), :],
            self.perm[plane, :, pl.ds(row, rows), :],
            self.spacing,
        )

    def make_ty(self, plane, row, rows):
        here = self.perm[plane, :, pl.ds(row, rows), :]
        lane = lax.broadcasted_iota(jnp.int32, here.shape, 2)
        block = lax.broadcasted_iota(jnp.int32, here.shape, 0)
        last = (lane == LANES - 1) & (block == here.shape[0] - 1)
        value = conduct(here, y_next(here), self.spacing)
        self.ty[plane, :, pl.ds(row, rows), :] = jnp.where(last, 0.0, value)

    def make_partial(self, plane, row, rows, faces):
        at, after = pl.ds(row, rows), pl.ds(row + 1, rows)
        along = self.ty[plane, :, at, :]
        total = self.storage + self.tz[plane, :, at, :] + self.tz[plane, :, after, :]
        total = total + along + y_prev(along)
        for face in faces:
            total = total + self.tx[face, :, at, :]
        return total

    def set_diag(self, plane, row, rows, total):
        at = pl.ds(row, rows)
        if self.diag is not None:
            self.diag[plane, :, at, :] = total
        self.inv[plane, :, at, :] = jnp.where(self.perm[plane, :, at, :] > 0.0, 0.8 / total, 0.0)

    def make_diag(self, plane, row, rows):
        self.set_diag(plane, row, rows, self.make_partial(plane, row, rows, (plane, plane + 1)))

    def flow(self, field, plane, row, rows):
        at, after = pl.ds(row, rows), pl.ds(row + 1, rows)
        here = field[plane, :, at, :]
        along = self.ty[plane, :, at, :]
        total = self.tx[plane, :, at, :] * field[plane - 1, :, at, :]
        total = total + self.tx[plane + 1, :, at, :] * field[plane + 1, :, at, :]
        total = total + self.tz[plane, :, at, :] * field[plane, :, pl.ds(row - 1, rows), :]
        total = total + self.tz[plane, :, after, :] * field[plane, :, after, :]
        total = total + along * y_next(here) + y_prev(along * here)
        return here, total


def take(values, index):
    return jnp.take_along_axis(values, index, axis=1, mode="promise_in_bounds")


def coarsen(ref, plane, block, row, rows):
    lane = lax.broadcasted_iota(jnp.int32, (rows, LANES), 1)
    index = lax.rem(2 * lane, LANES)
    parts = []
    for half in (0, 1):
        total = None
        for step_x in (0, 1):
            for step_z in (0, 1):
                piece = ref[plane + step_x, 2 * block + half, pl.ds(row + step_z, rows, stride=2), :]
                total = piece if total is None else total + piece
        parts.append(take(total + pltpu.roll(total, LANES - 1, 1), index))
    return jnp.where(lane < LANES // 2, parts[0], parts[1])


def refine_rows(target, target_plane, target_block, values):
    rows = values.shape[0]
    lane = lax.broadcasted_iota(jnp.int32, values.shape, 1)
    spread = take(values, (LANES // 2) * (target_block % 2) + lane // 2)
    target[target_plane, target_block, pl.ds(0, rows, stride=2), :] = spread
    target[target_plane, target_block, pl.ds(1, rows, stride=2), :] = spread


def kernel(
    n_wide, n_narrow,
    pressure, source, permeability, active_mask, out,
    raw, act, rhs, v0, v1, v2, v3, perm, tx, tz, ty, diag, inv, resid,
    zs1, zr1, zs2, zr2, zs3, zr3,
    m_raw, m_perm, m_tx, m_tz, m_ty, m_diag, m_inv, m_rhs, m_f1, m_f2, m_u, m_fin, m_ref, m_corner, m_refz, m_res, rc, rf,
    c_perm, c_tx, c_tz, c_ty, c_inv, c_f1, c_f2, c_f3, c_f4,
    load_sem, send_sem, recv_sem,
):
    wide, narrow = lax.axis_index("wide"), lax.axis_index("narrow")
    fine = Level(1.0, perm, tx, tz, ty, diag, inv)
    mid = Level(2.0, m_perm, m_tx, m_tz, m_ty, m_diag, m_inv)
    coarse = Level(4.0, c_perm, c_tx, c_tz, c_ty, None, c_inv)
    slots = [0]

    def exists(dx, dz):
        ok = None
        for step, here, count in ((dx, wide, n_wide), (dz, narrow, n_narrow)):
            if step == 0:
                continue
            one = here + step < count if step > 0 else here + step >= 0
            ok = one if ok is None else ok & one
        return ok

    odd = lax.rem(wide, 2)
    chip_step, off_step = 1 - 2 * odd, 2 * odd - 1
    off_ok = ((odd == 1) & (wide + 1 < n_wide)) | ((odd == 0) & (wide > 0))
    near, far = 4 - 3 * odd, 1 + 3 * odd
    near_face, far_face = 5 - 4 * odd, 1 + 4 * odd
    chip_at, off_at = 5 * odd, 5 - 5 * odd
    mid_near, mid_far = 3 - odd, 2 + odd
    everyone = []

    def swap(ok, back, step_x, step_z, src, dst):
        slot = len(everyone)
        copy = pltpu.make_async_remote_copy(
            src_ref=src, dst_ref=dst, send_sem=send_sem.at[slot], recv_sem=recv_sem.at[slot],
            device_id=(wide + step_x, narrow + step_z), device_id_type=MESH,
        )
        everyone.append((ok, back, copy))
        return everyone[-1]

    def with_chip(src, dst, dz=0):
        if dz == 0:
            return swap(None, None, chip_step, 0, src, dst)
        return swap(exists(0, dz), exists(0, -dz), chip_step, dz, src, dst)

    def with_off(src, dst, dz=0):
        if dz == 0:
            return swap(off_ok, off_ok, off_step, 0, src, dst)
        return swap(off_ok & exists(0, dz), off_ok & exists(0, -dz), off_step, dz, src, dst)

    def with_z(dz, src, dst):
        return swap(exists(0, dz), exists(0, -dz), 0, dz, src, dst)

    def guarded(ok, act_on):
        if ok is None:
            act_on()
        else:
            pl.when(ok)(act_on)

    def start(group):
        for ok, _, copy in group:
            guarded(ok, copy.start)

    def wait(group):
        for _, back, copy in group:
            guarded(back, copy.wait_recv)

    peers = [(dx, dz) for dx in range(-REACH, REACH + 1) for dz in (-1, 0, 1) if (dx, dz) != (0, 0)]

    loads = []
    for which, (src, dst) in enumerate(
        ((permeability, raw), (active_mask, act), (pressure, v0), (source, rhs))
    ):
        for block in range(4):
            into = dst.at[pl.ds(1, 4), block, pl.ds(8, 64), :] if dst is v0 else dst.at[:, block, :, :]
            copy = pltpu.make_async_copy(
                src.at[:, :, pl.ds(block * LANES, LANES)], into, load_sem.at[which * 4 + block]
            )
            copy.start()
            loads.append(copy)

    for ref in (m_perm, m_f1, m_ref, m_corner, m_refz, c_perm, c_f1, zr1, zr2, zr3):
        ref[...] = jnp.zeros(ref.shape, F32)
    for ref in (m_u, m_f2, c_f2, c_f3):
        ref[...] = jnp.zeros(ref.shape, F32)

    barrier = pltpu.get_barrier_semaphore()
    for dx, dz in peers:
        @pl.when(exists(dx, dz))
        def _():
            pl.semaphore_signal(barrier, inc=1, device_id=(wide + dx, narrow + dz), device_id_type=MESH)

    low_edge, high_edge = wide == 0, wide == n_wide - 1
    for plane, edge in ((0, low_edge), (5, high_edge)):
        @pl.when(edge)
        def _():
            for ref in (perm, v0, v1, v2):
                ref[plane] = jnp.zeros(ref.shape[1:], F32)

    def chunks(first, last, body):
        def step(k, carry):
            body(pl.multiple_of(k * 8, 8))
            return carry
        lax.fori_loop(first // 8, last // 8, step, 0)

    for copy in loads[:8]:
        copy.wait()

    def mask_perm(row):
        for plane in range(4):
            value = raw[plane, :, pl.ds(row, 8), :] * act[plane, :, pl.ds(row, 8), :].astype(F32)
            perm[plane + 1, :, pl.ds(row + 8, 8), :] = value

    chunks(0, 64, mask_perm)
    for copy in loads[8:12]:
        copy.wait()

    def pack(target, field):
        for side, row in ((0, 8), (1, 71)):
            for plane in range(4):
                for block in range(4):
                    target[side, pl.ds(plane * 4 + block, 1), :] = field[plane + 1, block, pl.ds(row, 1), :]

    def unpack(field, buffer):
        for side, row in ((0, 7), (1, 72)):
            for plane in range(4):
                for block in range(4):
                    field[plane + 1, block, pl.ds(row, 1), :] = buffer[side, pl.ds(plane * 4 + block, 1), :]

    pieces = (0, 3, 1, 2)

    def fine_chip(field):
        rows = pl.ds(8, 64)
        return [with_chip(field.at[near, :, rows, :], field.at[chip_at, :, rows, :])]

    def fine_off(field):
        made = {}
        for piece in pieces:
            rows = pl.ds(8 + 16 * piece, 16)
            made[piece] = [with_off(field.at[far, :, rows, :], field.at[off_at, :, rows, :])]
        return made

    def fine_z(send, recv):
        return [with_z(-1, send.at[0], recv.at[1]), with_z(1, send.at[1], recv.at[0])]

    pack(zs1.at[0], perm)
    pack(zs1.at[1], v0)

    count_x = jnp.minimum(wide, REACH) + jnp.minimum(n_wide - 1 - wide, REACH) + 1
    count_z = jnp.minimum(narrow, 1) + jnp.minimum(n_narrow - 1 - narrow, 1) + 1
    pl.semaphore_wait(barrier, count_x * count_z - 1)

    perm_chip, v0_chip = fine_chip(perm), fine_chip(v0)
    perm_off, v0_off = fine_off(perm), fine_off(v0)
    perm_z = fine_z(zs1.at[0], zr1.at[0])
    v0_z = fine_z(zs1.at[1], zr1.at[1])
    start(perm_chip + v0_chip)
    start(perm_z + v0_z)
    for piece in pieces:
        start(perm_off[piece] + v0_off[piece])

    for plane in range(2):
        for block in range(2):
            value = coarsen(raw, 2 * plane, block, 0, 32) * 0.125
            m_raw[plane, block] = value
            some = coarsen(perm, 2 * plane + 1, block, 8, 32) > 0.0
            m_perm[plane + 2, block, pl.ds(16, 32), :] = jnp.where(some, value, 0.0)

    def mid_swaps(ref):
        own, low, high = pl.ds(16, 32), pl.ds(16, 8), pl.ds(40, 8)
        below, above = pl.ds(8, 8), pl.ds(48, 8)
        groups = []
        for plane in (mid_near, mid_far):
            over, back = plane + 2 - 4 * odd, plane - 2 + 4 * odd
            group = [
                with_off(ref.at[plane, :, own, :], ref.at[over, :, own, :]),
                with_chip(ref.at[plane, :, own, :], ref.at[back, :, own, :]),
                with_z(-1, ref.at[plane, :, low, :], ref.at[plane, :, above, :]),
                with_z(1, ref.at[plane, :, high, :], ref.at[plane, :, below, :]),
            ]
            cross, there = (with_chip, back) if plane is mid_near else (with_off, over)
            group.append(cross(ref.at[plane, :, low, :], ref.at[there, :, above, :], -1))
            group.append(cross(ref.at[plane, :, high, :], ref.at[there, :, below, :], 1))
            groups.append(group)
        return groups

    def coarse_swaps(ref):
        mine = {0: pl.ds(16, 16), -1: pl.ds(16, 8), 1: pl.ds(24, 8)}
        theirs = {0: pl.ds(16, 16), -1: pl.ds(32, 8), 1: pl.ds(8, 8)}
        return [
            swap(exists(dx, dz), exists(-dx, -dz), dx, dz, ref.at[4, :, mine[dz], :], ref.at[4 - dx, :, theirs[dz], :])
            for dx, dz in sorted(peers, key=lambda one: -abs(one[0]))
        ]

    mid_perm_near, mid_perm_far = mid_swaps(m_perm)
    some = coarsen(m_perm, 2, 0, 16, 16) > 0.0
    value = coarsen(m_raw, 0, 0, 0, 16) * 0.125
    c_perm[4, 0, pl.ds(16, 16), :] = jnp.where(some, value, 0.0)
    coarse_perm_swaps = coarse_swaps(c_perm)

    def inner(row):
        for plane in range(1, 5):
            fine.make_ty(plane, row, 8)
            if plane > 1:
                fine.make_tx(plane, row, 8)

    chunks(8, 72, inner)

    def inner_z(row):
        for plane in range(1, 5):
            fine.make_tz(plane, row, 8)

    chunks(16, 72, inner_z)
    inside = (near, 2, 3)

    def relax(old, new, plane, row, first):
        at = pl.ds(row, 8)
        here, total = fine.flow(old, plane, row, 8)
        if first:
            here = jnp.where(perm[plane, :, at, :] > 0.0, here, 0.0)
        force = rhs[plane - 1, :, pl.ds(row - 8, 8), :] + total
        new[plane, :, at, :] = 0.2 * here + inv[plane, :, at, :] * force

    def residual(plane, row):
        at = pl.ds(row, 8)
        here, total = fine.flow(v2, plane, row, 8)
        value = rhs[plane - 1, :, pl.ds(row - 8, 8), :] + total - diag[plane, :, at, :] * here
        resid[plane - 1, :, pl.ds(row - 8, 8), :] = jnp.where(perm[plane, :, at, :] > 0.0, value, 0.0)

    wait(perm_chip)
    chunks(8, 72, lambda row: fine.make_tx(near_face, row, 8))
    wait(perm_z + v0_z)
    unpack(perm, zr1.at[0])
    unpack(v0, zr1.at[1])
    inner_z(8)
    inner_z(72)
    for copy in loads[12:]:
        copy.wait()

    def inside_diag(row):
        for plane in inside:
            fine.make_diag(plane, row, 8)
        diag[far, :, pl.ds(row, 8), :] = fine.make_partial(far, row, 8, (2 + 2 * odd,))

    chunks(8, 72, inside_diag)
    wait(v0_chip)

    v1_chip, v1_off, v1_z = fine_chip(v1), fine_off(v1), fine_z(zs2, zr2)
    v2_chip, v2_off, v2_z = fine_chip(v2), fine_off(v2), fine_z(zs3, zr3)
    mid_f1_near, mid_f1_far = mid_swaps(m_f1)

    def relax_inside(old, new, first, rows):
        def body(row):
            for plane in inside:
                relax(old, new, plane, row, first)
        for low, high in rows:
            chunks(low, high, body)

    relax_inside(v0, v1, True, ((8, 72),))
    start(v1_chip)
    for piece in pieces:
        wait(perm_off[piece] + v0_off[piece])
        for row in (8 + 16 * piece, 16 + 16 * piece):
            fine.make_tx(far_face, row, 8)
            fine.set_diag(far, row, 8, diag[far, :, pl.ds(row, 8), :] + tx[far_face, :, pl.ds(row, 8), :])
            relax(v0, v1, far, row, True)
        start(v1_off[piece])
        if piece == 3:
            pack(zs2, v1)
            start(v1_z)
    start(mid_perm_near + mid_perm_far)

    wait(v1_chip)
    relax_inside(v1, v2, False, ((16, 64),))
    wait(v1_z)
    unpack(v1, zr2)
    relax_inside(v1, v2, False, ((8, 16), (64, 72)))
    start(v2_chip)
    for piece in pieces:
        wait(v1_off[piece])
        for row in (8 + 16 * piece, 16 + 16 * piece):
            relax(v1, v2, far, row, False)
        start(v2_off[piece])
        if piece == 3:
            pack(zs3, v2)
            start(v2_z)
    start(coarse_perm_swaps)

    wait(mid_perm_near + mid_perm_far)
    for plane in range(1, 6):
        mid.make_tx(plane, 8, 48)
    for plane in range(1, 5):
        mid.make_ty(plane, 8, 48)
        mid.make_tz(plane, 8, 56)
        mid.make_diag(plane, 8, 48)

    own = pl.ds(16, 32)

    def mid_first(plane):
        for block in range(2):
            value = coarsen(resid, 2 * (plane - 2), block, 0, 32)
            value = jnp.where(m_perm[plane, block, own, :] > 0.0, value, 0.0)
            m_rhs[plane - 2, block] = value
            m_f1[plane, block, own, :] = m_inv[plane, block, own, :] * value

    def inside_residual(row):
        for plane in inside:
            residual(plane, row)

    wait(v2_chip)
    chunks(16, 64, inside_residual)
    wait(v2_z)
    unpack(v2, zr3)
    chunks(8, 16, inside_residual)
    chunks(64, 72, inside_residual)
    mid_first(mid_near)
    start(mid_f1_near)
    for piece in pieces:
        wait(v2_off[piece])
        for row in (8 + 16 * piece, 16 + 16 * piece):
            residual(far, row)
    mid_first(mid_far)
    start(mid_f1_far)

    wait(coarse_perm_swaps)
    for plane in range(1, 9):
        coarse.make_tx(plane, 8, 32)
    for plane in range(1, 8):
        coarse.make_ty(plane, 8, 32)
        coarse.make_tz(plane, 8, 40)
        coarse.make_diag(plane, 8, 32)

    wait(mid_f1_near + mid_f1_far)
    for plane in range(1, 5):
        here, total = mid.flow(m_f1, plane, 8, 48)
        m_f2[plane, :, pl.ds(8, 48), :] = 1.2 * here + m_inv[plane, :, pl.ds(8, 48), :] * total
    for plane in range(2):
        here, total = mid.flow(m_f2, plane + 2, 16, 32)
        value = m_rhs[plane] + total - m_diag[plane + 2, :, own, :] * here
        m_res[plane] = jnp.where(m_perm[plane + 2, :, own, :] > 0.0, value, 0.0)

    here = pl.ds(16, 16)
    value = coarsen(m_res, 0, 0, 0, 16)
    c_f1[4, 0, here, :] = c_inv[4, 0, here, :] * value
    coarse_f1_swaps = coarse_swaps(c_f1)
    start(coarse_f1_swaps)
    tall = pl.ds(8, 48)
    two, low, high = pl.ds(2, 2), pl.ds(8, 8), pl.ds(48, 8)
    mid_f2_swaps = [
        with_off(m_f2.at[mid_near, :, own, :], m_ref.at[1 - odd]),
        with_off(m_f2.at[mid_far, :, low, :], m_corner.at[1 - odd, 0]),
        with_off(m_f2.at[mid_far, :, high, :], m_corner.at[1 - odd, 1]),
        with_chip(m_f2.at[mid_far, :, own, :], m_ref.at[odd]),
        with_chip(m_f2.at[mid_near, :, low, :], m_corner.at[odd, 0]),
        with_chip(m_f2.at[mid_near, :, high, :], m_corner.at[odd, 1]),
        with_z(-1, m_f2.at[two, :, pl.ds(16, 8), :], m_refz.at[1]),
        with_z(1, m_f2.at[two, :, pl.ds(40, 8), :], m_refz.at[0]),
    ]
    start(mid_f2_swaps)
    wait(coarse_f1_swaps)
    body = pl.ds(8, 32)
    for old, new, first, last in ((c_f1, c_f2, 1, 7), (c_f2, c_f3, 2, 6), (c_f3, c_f4, 3, 5)):
        for plane in range(first, last + 1):
            value, total = coarse.flow(old, plane, 8, 32)
            value = 1.2 * value if old is c_f1 else 0.2 * value + c_f1[plane, :, body, :]
            new[plane, :, body, :] = value + c_inv[plane, :, body, :] * total

    for plane in range(3):
        for block in range(2):
            refine_rows(rc, plane, block, c_f4[plane + 3, 0, body, :])
    wait(mid_f2_swaps)
    for plane in range(6):
        for block in range(2):
            if plane in (0, 5):
                side = plane // 5
                add = jnp.where(m_perm[plane, block, own, :] > 0.0, rc[plane // 2, block, own, :], 0.0)
                m_u[plane, block, own, :] = m_ref[side, block] + add
                continue
            add = jnp.where(m_perm[plane, block, tall, :] > 0.0, rc[plane // 2, block, tall, :], 0.0)
            if plane in (2, 3):
                below, above = m_refz[0, plane - 2, block], m_refz[1, plane - 2, block]
            else:
                below, above = m_corner[plane // 4, 0, block], m_corner[plane // 4, 1, block]
            m_u[plane, block, tall, :] = jnp.concatenate([below, m_f2[plane, block, own, :], above], 0) + add
    for plane in range(1, 5):
        value, total = mid.flow(m_u, plane, 8, 48)
        value = 0.2 * value + m_f1[plane, :, tall, :] + m_inv[plane, :, tall, :] * total
        m_fin[plane, :, tall, :] = value

    for plane in range(4):
        for block in range(4):
            refine_rows(rf, plane, block, m_fin[plane + 1, block // 2, pl.ds(12, 40), :])

    def correct(row):
        at = pl.ds(row, 8)
        for plane in range(6):
            add = jnp.where(perm[plane, :, at, :] > 0.0, rf[(plane + 1) // 2, :, at, :], 0.0)
            v3[plane, :, at, :] = v2[plane, :, at, :] + add

    chunks(0, 80, correct)

    def finish(row):
        at = pl.ds(row, 8)
        for plane in range(1, 5):
            value, total = fine.flow(v3, plane, row, 8)
            force = rhs[plane - 1, :, pl.ds(row - 8, 8), :] + total
            value = 0.2 * value + inv[plane, :, at, :] * force
            for block in range(4):
                out[plane - 1, pl.ds(pl.multiple_of(row - 8, 8), 8), pl.ds(block * LANES, LANES)] = value[block]

    chunks(8, 72, finish)
    for ok, _, copy in everyone:
        guarded(ok, copy.wait_send)


def per_device(n_wide, n_narrow, pressure, source, permeability, active_mask):
    def vmem(*shape, dtype=F32):
        return pltpu.VMEM(shape, dtype)

    fine_pad, fine_own = (6, 4, 80, LANES), (4, 4, 64, LANES)
    mid_pad, mid_own = (6, 2, 64, LANES), (2, 2, 32, LANES)
    coarse_pad = (9, 1, 48, LANES)
    scratch = [vmem(*fine_own), vmem(*fine_own, dtype=jnp.int32), vmem(*fine_own)]
    scratch += [vmem(*fine_pad) for _ in range(10)] + [vmem(*fine_own)]
    scratch += [vmem(2, 2, 16, LANES), vmem(2, 2, 16, LANES)] + [vmem(2, 16, LANES) for _ in range(4)]
    scratch += [vmem(*mid_own)] + [vmem(*mid_pad) for _ in range(6)] + [vmem(*mid_own)]
    scratch += [vmem(*mid_pad) for _ in range(4)]
    scratch += [vmem(2, 2, 32, LANES), vmem(2, 2, 2, 8, LANES), vmem(2, 2, 2, 8, LANES), vmem(*mid_own)]
    scratch += [vmem(3, 2, 64, LANES), vmem(4, 4, 80, LANES)]
    scratch += [vmem(*coarse_pad) for _ in range(9)]
    scratch += [pltpu.SemaphoreType.DMA((16,)), pltpu.SemaphoreType.DMA((128,)), pltpu.SemaphoreType.DMA((128,))]
    return pl.pallas_call(
        functools.partial(kernel, n_wide, n_narrow),
        out_shape=jax.ShapeDtypeStruct(pressure.shape, F32),
        in_specs=[pl.BlockSpec(memory_space=pl.ANY)] * 4,
        out_specs=pl.BlockSpec(memory_space=pltpu.VMEM),
        scratch_shapes=scratch,
        compiler_params=pltpu.CompilerParams(
            collective_id=0, has_side_effects=True, vmem_limit_bytes=67043328
        ),
        name="vcycle",
    )(pressure, source, permeability, active_mask)


def solution(mesh):
    spec = P("wide", "narrow", None)
    return jax.shard_map(
        functools.partial(per_device, mesh.shape["wide"], mesh.shape["narrow"]),
        mesh=mesh, in_specs=(spec,) * 4, out_specs=spec, check_vma=False,
    )
```

```python
import functools

import jax
import jax.numpy as jnp
from jax import lax
from jax.experimental import pallas as pl
from jax.experimental.pallas import tpu as pltpu
from jax.sharding import PartitionSpec as P

FLOOR_SUM = 0.1
LANES = 128
F32 = jnp.float32
MESH = pl.DeviceIdType.MESH

FINE_X, FINE_Z = 1, 8
MID_X, MID_Z = 2, 16
COARSE_X, COARSE_Z = 4, 16
REACH = 4


def y_next(values):
    rolled = pltpu.roll(values, LANES - 1, 2)
    if values.shape[0] == 1:
        return rolled
    lane = lax.broadcasted_iota(jnp.int32, values.shape, 2)
    return jnp.where(lane == LANES - 1, jnp.concatenate([rolled[1:], rolled[:1]], 0), rolled)


def y_prev(values):
    rolled = pltpu.roll(values, 1, 2)
    if values.shape[0] == 1:
        return rolled
    lane = lax.broadcasted_iota(jnp.int32, values.shape, 2)
    return jnp.where(lane == 0, jnp.concatenate([rolled[-1:], rolled[:-1]], 0), rolled)


def conduct(left, right, spacing):
    return (2.0 * spacing) * left * right / jnp.maximum(left + right, FLOOR_SUM)


class Level:
    def __init__(self, spacing, perm, tx, tz, ty, diag, inv):
        self.spacing, self.storage = spacing, 0.5 * spacing**3
        self.perm, self.tx, self.tz, self.ty = perm, tx, tz, ty
        self.diag, self.inv = diag, inv

    def make_tx(self, plane, row, rows):
        at = pl.ds(row, rows)
        self.tx[plane, :, at, :] = conduct(
            self.perm[plane - 1, :, at, :], self.perm[plane, :, at, :], self.spacing
        )

    def make_tz(self, plane, row, rows):
        self.tz[plane, :, pl.ds(row, rows), :] = conduct(
            self.perm[plane, :, pl.ds(row - 1, rows), :],
            self.perm[plane, :, pl.ds(row, rows), :],
            self.spacing,
        )

    def make_ty(self, plane, row, rows):
        here = self.perm[plane, :, pl.ds(row, rows), :]
        lane = lax.broadcasted_iota(jnp.int32, here.shape, 2)
        block = lax.broadcasted_iota(jnp.int32, here.shape, 0)
        last = (lane == LANES - 1) & (block == here.shape[0] - 1)
        value = conduct(here, y_next(here), self.spacing)
        self.ty[plane, :, pl.ds(row, rows), :] = jnp.where(last, 0.0, value)

    def make_partial(self, plane, row, rows, faces):
        at, after = pl.ds(row, rows), pl.ds(row + 1, rows)
        along = self.ty[plane, :, at, :]
        total = self.storage + self.tz[plane, :, at, :] + self.tz[plane, :, after, :]
        total = total + along + y_prev(along)
        for face in faces:
            total = total + self.tx[face, :, at, :]
        return total

    def set_diag(self, plane, row, rows, total):
        at = pl.ds(row, rows)
        if self.diag is not None:
            self.diag[plane, :, at, :] = total
        self.inv[plane, :, at, :] = jnp.where(self.perm[plane, :, at, :] > 0.0, 0.8 / total, 0.0)

    def make_diag(self, plane, row, rows):
        self.set_diag(plane, row, rows, self.make_partial(plane, row, rows, (plane, plane + 1)))

    def flow(self, field, plane, row, rows, planes=None):
        below, mine, above = planes or (plane - 1, plane, plane + 1)
        at, after = pl.ds(row, rows), pl.ds(row + 1, rows)
        here = field[mine, :, at, :]
        along = self.ty[plane, :, at, :]
        total = self.tx[plane, :, at, :] * field[below, :, at, :]
        total = total + self.tx[plane + 1, :, at, :] * field[above, :, at, :]
        total = total + self.tz[plane, :, at, :] * field[mine, :, pl.ds(row - 1, rows), :]
        total = total + self.tz[plane, :, after, :] * field[mine, :, after, :]
        total = total + along * y_next(here) + y_prev(along * here)
        return here, total


def take(values, index):
    return jnp.take_along_axis(values, index, axis=1, mode="promise_in_bounds")


def coarsen(ref, plane, block, row, rows):
    lane = lax.broadcasted_iota(jnp.int32, (rows, LANES), 1)
    index = lax.rem(2 * lane, LANES)
    parts = []
    for half in (0, 1):
        total = None
        for step_x in (0, 1):
            for step_z in (0, 1):
                piece = ref[plane + step_x, 2 * block + half, pl.ds(row + step_z, rows, stride=2), :]
                total = piece if total is None else total + piece
        parts.append(take(total + pltpu.roll(total, LANES - 1, 1), index))
    return jnp.where(lane < LANES // 2, parts[0], parts[1])


def refine_rows(target, target_plane, target_block, values):
    rows = values.shape[0]
    lane = lax.broadcasted_iota(jnp.int32, values.shape, 1)
    spread = take(values, (LANES // 2) * (target_block % 2) + lane // 2)
    target[target_plane, target_block, pl.ds(0, rows, stride=2), :] = spread
    target[target_plane, target_block, pl.ds(1, rows, stride=2), :] = spread


def kernel(
    n_wide, n_narrow,
    pressure, source, permeability, active_mask, out,
    raw, act, rhs, v0, v1, v2, v3, perm, tx, tz, ty, diag, inv, resid,
    zs1, zr1, zs2, zr2, zs3, zr3,
    m_raw, m_perm, m_tx, m_tz, m_ty, m_diag, m_inv, m_rhs, m_f1, m_f2, m_u, m_fin, m_ref, m_corner, m_refz, m_res, rc, rf,
    c_perm, c_tx, c_tz, c_ty, c_inv, c_f1, c_f2, c_f3, c_f4,
    load_sem, send_sem, recv_sem, hello,
):
    wide, narrow = lax.axis_index("wide"), lax.axis_index("narrow")
    fine = Level(1.0, perm, tx, tz, ty, diag, inv)
    mid = Level(2.0, m_perm, m_tx, m_tz, m_ty, m_diag, m_inv)
    coarse = Level(4.0, c_perm, c_tx, c_tz, c_ty, None, c_inv)
    slots = [0]

    def exists(dx, dz):
        ok = None
        for step, here, count in ((dx, wide, n_wide), (dz, narrow, n_narrow)):
            if step == 0:
                continue
            one = here + step < count if step > 0 else here + step >= 0
            ok = one if ok is None else ok & one
        return ok

    odd = lax.rem(wide, 2)
    chip_step, off_step = 1 - 2 * odd, 2 * odd - 1
    off_ok = ((odd == 1) & (wide + 1 < n_wide)) | ((odd == 0) & (wide > 0))
    near, far = 4 - 3 * odd, 1 + 3 * odd
    near_face, far_face = 5 - 4 * odd, 1 + 4 * odd
    chip_at, off_at = 5 * odd, 5 - 5 * odd
    mid_near, mid_far = 3 - odd, 2 + odd
    everyone = []

    def swap(ok, back, step_x, step_z, src, dst):
        slot = len(everyone)
        copy = pltpu.make_async_remote_copy(
            src_ref=src, dst_ref=dst, send_sem=send_sem.at[slot], recv_sem=recv_sem.at[slot],
            device_id=(wide + step_x, narrow + step_z), device_id_type=MESH,
        )
        everyone.append((ok, back, copy))
        return everyone[-1]

    def with_chip(src, dst, dz=0):
        if dz == 0:
            return swap(None, None, chip_step, 0, src, dst)
        return swap(exists(0, dz), exists(0, -dz), chip_step, dz, src, dst)

    def with_off(src, dst, dz=0):
        if dz == 0:
            return swap(off_ok, off_ok, off_step, 0, src, dst)
        return swap(off_ok & exists(0, dz), off_ok & exists(0, -dz), off_step, dz, src, dst)

    def with_z(dz, src, dst):
        return swap(exists(0, dz), exists(0, -dz), 0, dz, src, dst)

    def guarded(ok, act_on):
        if ok is None:
            act_on()
        else:
            pl.when(ok)(act_on)

    def start(group):
        for ok, _, copy in group:
            guarded(ok, copy.start)

    def wait(group):
        for _, back, copy in group:
            guarded(back, copy.wait_recv)

    peers = [(dx, dz) for dx in range(-REACH, REACH + 1) for dz in (-1, 0, 1) if (dx, dz) != (0, 0)]

    loads = []
    for which, (src, dst) in enumerate(
        ((permeability, raw), (active_mask, act), (pressure, v0), (source, rhs))
    ):
        for block in range(4):
            into = dst.at[pl.ds(1, 4), block, pl.ds(8, 64), :] if dst is v0 else dst.at[:, block, :, :]
            copy = pltpu.make_async_copy(
                src.at[:, :, pl.ds(block * LANES, LANES)], into, load_sem.at[which * 4 + block]
            )
            copy.start()
            loads.append(copy)

    for ref in (m_perm, m_f1, m_ref, m_corner, m_refz, c_perm, c_f1, zr1, zr2, zr3):
        ref[...] = jnp.zeros(ref.shape, F32)
    for ref in (m_u, m_f2, c_f2, c_f3):
        ref[...] = jnp.zeros(ref.shape, F32)

    barrier = pltpu.get_barrier_semaphore()
    for dx, dz in ((1, 0), (-1, 0), (0, 1), (0, -1)):
        @pl.when(exists(dx, dz))
        def _():
            pl.semaphore_signal(barrier, inc=1, device_id=(wide + dx, narrow + dz), device_id_type=MESH)

    low_edge, high_edge = wide == 0, wide == n_wide - 1
    for plane, edge in ((0, low_edge), (5, high_edge)):
        @pl.when(edge)
        def _():
            for ref in (perm, v0, v1, v2):
                ref[plane] = jnp.zeros(ref.shape[1:], F32)

    def chunks(first, last, body):
        def step(k, carry):
            body(pl.multiple_of(k * 8, 8))
            return carry
        lax.fori_loop(first // 8, last // 8, step, 0)

    for copy in loads[:8]:
        copy.wait()

    def mask_perm(row):
        for plane in range(4):
            value = raw[plane, :, pl.ds(row, 8), :] * act[plane, :, pl.ds(row, 8), :].astype(F32)
            perm[plane + 1, :, pl.ds(row + 8, 8), :] = value

    chunks(0, 64, mask_perm)
    for copy in loads[8:12]:
        copy.wait()

    def pack(target, field):
        for side, row in ((0, 8), (1, 71)):
            for plane in range(4):
                for block in range(4):
                    target[side, pl.ds(plane * 4 + block, 1), :] = field[plane + 1, block, pl.ds(row, 1), :]

    def unpack(field, buffer):
        for side, row in ((0, 7), (1, 72)):
            for plane in range(4):
                for block in range(4):
                    field[plane + 1, block, pl.ds(row, 1), :] = buffer[side, pl.ds(plane * 4 + block, 1), :]

    def greet(turn):
        pl.semaphore_signal(
            hello.at[turn], inc=1, device_id=(wide + chip_step, narrow), device_id_type=MESH
        )

    def greeted(turn):
        pl.semaphore_wait(hello.at[turn], 1)

    pieces = (0, 3, 1, 2)

    def fine_chip(field):
        rows = pl.ds(8, 64)
        return [with_chip(field.at[near, :, rows, :], field.at[chip_at, :, rows, :])]

    def fine_off(field):
        made = {}
        for piece in pieces:
            rows = pl.ds(8 + 16 * piece, 16)
            made[piece] = [with_off(field.at[far, :, rows, :], field.at[off_at, :, rows, :])]
        return made

    def fine_z(send, recv):
        return [with_z(-1, send.at[0], recv.at[1]), with_z(1, send.at[1], recv.at[0])]

    pack(zs1.at[0], perm)
    pack(zs1.at[1], v0)

    count_x = jnp.minimum(wide, 1) + jnp.minimum(n_wide - 1 - wide, 1)
    count_z = jnp.minimum(narrow, 1) + jnp.minimum(n_narrow - 1 - narrow, 1)
    pl.semaphore_wait(barrier, count_x + count_z)

    perm_chip, v0_chip = fine_chip(perm), fine_chip(v0)
    perm_off, v0_off = fine_off(perm), fine_off(v0)
    perm_z = fine_z(zs1.at[0], zr1.at[0])
    v0_z = fine_z(zs1.at[1], zr1.at[1])
    start(perm_chip + v0_chip)
    start(perm_z + v0_z)
    for piece in pieces:
        start(perm_off[piece] + v0_off[piece])

    for plane in range(2):
        for block in range(2):
            value = coarsen(raw, 2 * plane, block, 0, 32) * 0.125
            m_raw[plane, block] = value
            some = coarsen(perm, 2 * plane + 1, block, 8, 32) > 0.0
            m_perm[plane + 2, block, pl.ds(16, 32), :] = jnp.where(some, value, 0.0)

    def mid_swaps(ref):
        own, low, high = pl.ds(16, 32), pl.ds(16, 8), pl.ds(40, 8)
        below, above = pl.ds(8, 8), pl.ds(48, 8)
        groups = []
        for plane in (mid_near, mid_far):
            over, back = plane + 2 - 4 * odd, plane - 2 + 4 * odd
            group = [
                with_off(ref.at[plane, :, own, :], ref.at[over, :, own, :]),
                with_chip(ref.at[plane, :, own, :], ref.at[back, :, own, :]),
                with_z(-1, ref.at[plane, :, low, :], ref.at[plane, :, above, :]),
                with_z(1, ref.at[plane, :, high, :], ref.at[plane, :, below, :]),
            ]
            cross, there = (with_chip, back) if plane is mid_near else (with_off, over)
            group.append(cross(ref.at[plane, :, low, :], ref.at[there, :, above, :], -1))
            group.append(cross(ref.at[plane, :, high, :], ref.at[there, :, below, :], 1))
            groups.append(group)
        return groups

    def coarse_swaps(ref):
        mine = {0: pl.ds(16, 16), -1: pl.ds(16, 8), 1: pl.ds(24, 8)}
        theirs = {0: pl.ds(16, 16), -1: pl.ds(32, 8), 1: pl.ds(8, 8)}
        groups = ([], [], [])
        for dx, dz in sorted(peers, key=lambda one: -abs(one[0])):
            one = swap(
                exists(dx, dz), exists(-dx, -dz), dx, dz,
                ref.at[4, :, mine[dz], :], ref.at[4 - dx, :, theirs[dz], :],
            )
            groups[max(abs(dx) + abs(dz), 3) - 3].append(one)
        return groups

    mid_perm_near, mid_perm_far = mid_swaps(m_perm)
    some = coarsen(m_perm, 2, 0, 16, 16) > 0.0
    value = coarsen(m_raw, 0, 0, 0, 16) * 0.125
    c_perm[4, 0, pl.ds(16, 16), :] = jnp.where(some, value, 0.0)
    coarse_perm_swaps = coarse_swaps(c_perm)

    def inner(row):
        for plane in range(1, 5):
            fine.make_ty(plane, row, 8)
            if plane > 1:
                fine.make_tx(plane, row, 8)

    chunks(8, 72, inner)

    def inner_z(row):
        for plane in range(1, 5):
            fine.make_tz(plane, row, 8)

    chunks(16, 72, inner_z)
    inside = (near, 2, 3)

    def relax(old, new, plane, row, first):
        at = pl.ds(row, 8)
        here, total = fine.flow(old, plane, row, 8)
        if first:
            here = jnp.where(perm[plane, :, at, :] > 0.0, here, 0.0)
        force = rhs[plane - 1, :, pl.ds(row - 8, 8), :] + total
        new[plane, :, at, :] = 0.2 * here + inv[plane, :, at, :] * force

    def residual(plane, row):
        at = pl.ds(row, 8)
        here, total = fine.flow(v2, plane, row, 8)
        value = rhs[plane - 1, :, pl.ds(row - 8, 8), :] + total - diag[plane, :, at, :] * here
        resid[plane - 1, :, pl.ds(row - 8, 8), :] = jnp.where(perm[plane, :, at, :] > 0.0, value, 0.0)

    wait(perm_chip)
    chunks(8, 72, lambda row: fine.make_tx(near_face, row, 8))
    wait(perm_z + v0_z)
    unpack(perm, zr1.at[0])
    unpack(v0, zr1.at[1])
    inner_z(8)
    inner_z(72)
    for copy in loads[12:]:
        copy.wait()

    def inside_diag(row):
        for plane in inside:
            fine.make_diag(plane, row, 8)
        diag[far, :, pl.ds(row, 8), :] = fine.make_partial(far, row, 8, (2 + 2 * odd,))

    chunks(8, 72, inside_diag)
    wait(v0_chip)

    v1_chip, v1_off, v1_z = fine_chip(v1), fine_off(v1), fine_z(zs2, zr2)
    v2_chip, v2_off, v2_z = fine_chip(v2), fine_off(v2), fine_z(zs3, zr3)
    mid_f1_near, mid_f1_far = mid_swaps(m_f1)

    def relax_inside(old, new, first, rows):
        def body(row):
            for plane in inside:
                relax(old, new, plane, row, first)
        for low, high in rows:
            chunks(low, high, body)

    relax_inside(v0, v1, True, ((8, 72),))
    start(v1_chip)
    for piece in pieces:
        wait(perm_off[piece] + v0_off[piece])
        for row in (8 + 16 * piece, 16 + 16 * piece):
            fine.make_tx(far_face, row, 8)
            fine.set_diag(far, row, 8, diag[far, :, pl.ds(row, 8), :] + tx[far_face, :, pl.ds(row, 8), :])
            relax(v0, v1, far, row, True)
        start(v1_off[piece])
        if piece == 3:
            pack(zs2, v1)
            start(v1_z)
    start(mid_perm_near + mid_perm_far)
    greet(0)

    wait(v1_chip)
    relax_inside(v1, v2, False, ((16, 64),))
    wait(v1_z)
    unpack(v1, zr2)
    relax_inside(v1, v2, False, ((8, 16), (64, 72)))
    start(v2_chip)
    greeted(0)
    for piece in pieces:
        wait(v1_off[piece])
        for row in (8 + 16 * piece, 16 + 16 * piece):
            relax(v1, v2, far, row, False)
        start(v2_off[piece])
        if piece == 3:
            pack(zs3, v2)
            start(v2_z)
    start(coarse_perm_swaps[0])
    greet(1)

    wait(mid_perm_near + mid_perm_far)
    for plane in range(1, 6):
        mid.make_tx(plane, 8, 48)
    for plane in range(1, 5):
        mid.make_ty(plane, 8, 48)
        mid.make_tz(plane, 8, 56)
        mid.make_diag(plane, 8, 48)

    own = pl.ds(16, 32)

    def mid_first(plane):
        for block in range(2):
            value = coarsen(resid, 2 * (plane - 2), block, 0, 32)
            value = jnp.where(m_perm[plane, block, own, :] > 0.0, value, 0.0)
            m_rhs[plane - 2, block] = value
            m_f1[plane, block, own, :] = m_inv[plane, block, own, :] * value

    def inside_residual(row):
        for plane in inside:
            residual(plane, row)

    wait(v2_chip)
    chunks(16, 64, inside_residual)
    wait(v2_z)
    unpack(v2, zr3)
    chunks(8, 16, inside_residual)
    chunks(64, 72, inside_residual)
    mid_first(mid_near)
    start(mid_f1_near)
    for piece in pieces:
        wait(v2_off[piece])
        for row in (8 + 16 * piece, 16 + 16 * piece):
            residual(far, row)
    mid_first(mid_far)
    greeted(1)
    start(mid_f1_far)
    start(coarse_perm_swaps[1])

    def coarse_faces(group, faces, planes, diags):
        wait(group)
        for plane in faces:
            coarse.make_tx(plane, 8, 32)
        for plane in planes:
            coarse.make_ty(plane, 8, 32)
            coarse.make_tz(plane, 8, 40)
        for plane in diags:
            coarse.make_diag(plane, 8, 32)

    coarse_faces(coarse_perm_swaps[0], range(3, 7), range(2, 7), range(3, 6))
    wait(mid_f1_near + mid_f1_far)
    for plane in range(1, 5):
        here, total = mid.flow(m_f1, plane, 8, 48)
        m_f2[plane, :, pl.ds(8, 48), :] = 1.2 * here + m_inv[plane, :, pl.ds(8, 48), :] * total
    for plane in range(2):
        here, total = mid.flow(m_f2, plane + 2, 16, 32)
        value = m_rhs[plane] + total - m_diag[plane + 2, :, own, :] * here
        m_res[plane] = jnp.where(m_perm[plane + 2, :, own, :] > 0.0, value, 0.0)

    here = pl.ds(16, 16)
    value = coarsen(m_res, 0, 0, 0, 16)
    c_f1[4, 0, here, :] = c_inv[4, 0, here, :] * value
    coarse_f1_swaps = coarse_swaps(c_f1)
    coarse_f1_swaps = coarse_f1_swaps[2] + coarse_f1_swaps[1] + coarse_f1_swaps[0]
    start(coarse_f1_swaps + coarse_perm_swaps[2])
    tall = pl.ds(8, 48)
    two, low, high = pl.ds(2, 2), pl.ds(8, 8), pl.ds(48, 8)
    mid_f2_swaps = [
        with_off(m_f2.at[mid_near, :, own, :], m_ref.at[1 - odd]),
        with_off(m_f2.at[mid_far, :, low, :], m_corner.at[1 - odd, 0]),
        with_off(m_f2.at[mid_far, :, high, :], m_corner.at[1 - odd, 1]),
        with_chip(m_f2.at[mid_far, :, own, :], m_ref.at[odd]),
        with_chip(m_f2.at[mid_near, :, low, :], m_corner.at[odd, 0]),
        with_chip(m_f2.at[mid_near, :, high, :], m_corner.at[odd, 1]),
        with_z(-1, m_f2.at[two, :, pl.ds(16, 8), :], m_refz.at[1]),
        with_z(1, m_f2.at[two, :, pl.ds(40, 8), :], m_refz.at[0]),
    ]
    start(mid_f2_swaps)

    def before_correction(row):
        for plane in range(1, 5):
            relax(v2, v3, plane, row, False)

    chunks(8, 72, before_correction)
    coarse_faces(coarse_perm_swaps[1], (2, 7), (1, 7), (2, 6))
    wait(coarse_f1_swaps)
    coarse_faces(coarse_perm_swaps[2], (1, 8), (), (1, 7))
    body = pl.ds(8, 32)
    for old, new, first, last in ((c_f1, c_f2, 1, 7), (c_f2, c_f3, 2, 6), (c_f3, c_f4, 3, 5)):
        for plane in range(first, last + 1):
            value, total = coarse.flow(old, plane, 8, 32)
            value = 1.2 * value if old is c_f1 else 0.2 * value + c_f1[plane, :, body, :]
            new[plane, :, body, :] = value + c_inv[plane, :, body, :] * total

    for plane in range(3):
        for block in range(2):
            refine_rows(rc, plane, block, c_f4[plane + 3, 0, body, :])
    wait(mid_f2_swaps)
    for plane in range(6):
        for block in range(2):
            if plane in (0, 5):
                side = plane // 5
                add = jnp.where(m_perm[plane, block, own, :] > 0.0, rc[plane // 2, block, own, :], 0.0)
                m_u[plane, block, own, :] = m_ref[side, block] + add
                continue
            add = jnp.where(m_perm[plane, block, tall, :] > 0.0, rc[plane // 2, block, tall, :], 0.0)
            if plane in (2, 3):
                below, above = m_refz[0, plane - 2, block], m_refz[1, plane - 2, block]
            else:
                below, above = m_corner[plane // 4, 0, block], m_corner[plane // 4, 1, block]
            m_u[plane, block, tall, :] = jnp.concatenate([below, m_f2[plane, block, own, :], above], 0) + add
    for plane in range(1, 5):
        value, total = mid.flow(m_u, plane, 8, 48)
        value = 0.2 * value + m_f1[plane, :, tall, :] + m_inv[plane, :, tall, :] * total
        m_fin[plane, :, tall, :] = value

    for plane in range(4):
        for block in range(4):
            refine_rows(rf, plane, block, m_fin[plane + 1, block // 2, pl.ds(12, 40), :])

    def finish(row):
        at = pl.ds(row, 8)
        for plane in range(1, 5):
            value, total = fine.flow(rf, plane, row, 8, (plane // 2, (plane + 1) // 2, (plane + 2) // 2))
            value = jnp.where(perm[plane, :, at, :] > 0.0, 0.2 * value, 0.0)
            value = v3[plane, :, at, :] + value + inv[plane, :, at, :] * total
            for block in range(4):
                out[plane - 1, pl.ds(pl.multiple_of(row - 8, 8), 8), pl.ds(block * LANES, LANES)] = value[block]

    chunks(8, 72, finish)
    for ok, _, copy in everyone:
        guarded(ok, copy.wait_send)


def per_device(n_wide, n_narrow, pressure, source, permeability, active_mask):
    def vmem(*shape, dtype=F32):
        return pltpu.VMEM(shape, dtype)

    fine_pad, fine_own = (6, 4, 80, LANES), (4, 4, 64, LANES)
    mid_pad, mid_own = (6, 2, 64, LANES), (2, 2, 32, LANES)
    coarse_pad = (9, 1, 48, LANES)
    scratch = [vmem(*fine_own), vmem(*fine_own, dtype=jnp.int32), vmem(*fine_own)]
    scratch += [vmem(*fine_pad) for _ in range(10)] + [vmem(*fine_own)]
    scratch += [vmem(2, 2, 16, LANES), vmem(2, 2, 16, LANES)] + [vmem(2, 16, LANES) for _ in range(4)]
    scratch += [vmem(*mid_own)] + [vmem(*mid_pad) for _ in range(6)] + [vmem(*mid_own)]
    scratch += [vmem(*mid_pad) for _ in range(4)]
    scratch += [vmem(2, 2, 32, LANES), vmem(2, 2, 2, 8, LANES), vmem(2, 2, 2, 8, LANES), vmem(*mid_own)]
    scratch += [vmem(3, 2, 64, LANES), vmem(4, 4, 80, LANES)]
    scratch += [vmem(*coarse_pad) for _ in range(9)]
    scratch += [pltpu.SemaphoreType.DMA((16,)), pltpu.SemaphoreType.DMA((128,)), pltpu.SemaphoreType.DMA((128,))]
    scratch += [pltpu.SemaphoreType.REGULAR((2,))]
    return pl.pallas_call(
        functools.partial(kernel, n_wide, n_narrow),
        out_shape=jax.ShapeDtypeStruct(pressure.shape, F32),
        in_specs=[pl.BlockSpec(memory_space=pl.ANY)] * 4,
        out_specs=pl.BlockSpec(memory_space=pltpu.VMEM),
        scratch_shapes=scratch,
        compiler_params=pltpu.CompilerParams(
            collective_id=0, has_side_effects=True, vmem_limit_bytes=48000000
        ),
        name="vcycle",
    )(*[pltpu.with_memory_space_constraint(x, pltpu.HBM) for x in (pressure, source, permeability, active_mask)])


def solution(mesh):
    spec = P("wide", "narrow", None)
    return jax.shard_map(
        functools.partial(per_device, mesh.shape["wide"], mesh.shape["narrow"]),
        mesh=mesh, in_specs=(spec,) * 4, out_specs=spec, check_vma=False,
    )
```
